32 devices in a mesh: row: 2 (over core), blk: 16 (over z, y, x).
Axes of the slice: x: 2, y: 2, z: 4, core: 2. Of those that a mesh axis runs over, the one named last changes fastest.
Arguments:
- state: float32 [2, 9, 5, 16, 2048], P('row', None, None, None, 'blk'), may hold values from -6 to 6
- inflow: float32 [9, 5, 2048], P(None, None, 'blk'), may hold values from -6 to 6
- blade_counts: int32 [2], replicated, may hold values from 20 to 60
- modes: int32 [1, 4], replicated, may hold values from 1 to 40
Outputs:
- advanced: float32 [2, 9, 5, 16, 2048], P('row', None, None, None, 'blk')
The draws below stay inside these ranges and needn't reach their ends.
All inputs are finite; a program needn't handle non-finite values.
Results may differ from the reference program's by a relative error of at most 0.0001.
Values sent between devices are 32-bit elements; how exact they have to be, the bound alone decides.
A program may use at most 64 MiB of HBM per device.

```python
import math
import jax
import jax.numpy as jnp
from jax import lax

VARS = 5
HARM = 4
CJ = 16
CT = 128
ROWS = 2
IFACES = 1
NT = 2048
N_BLK = 16


def with_ends(values, stream_key, least, high):
    longest = values.shape.index(max(values.shape))
    spots = []
    for shift in (0, 1):
        where = [jax.random.randint(jax.random.fold_in(stream_key, axis), (), 0, length) for axis, length in enumerate(values.shape)]
        where[longest] = (where[longest] + shift) % values.shape[longest]
        spots.append(tuple(where))
    return values.at[spots[0]].set(least).at[spots[1]].set(high)


def block_scale(stream_key, extent, cuts, least, high):
    factor_of, own = 1.0, jax.random.fold_in(stream_key, 6)
    for axis_at, blocks in cuts:
        heights = jnp.exp(jax.random.uniform(jax.random.fold_in(own, axis_at), (blocks,), jnp.float32, least / len(cuts), high / len(cuts)))
        factor_of = factor_of * jnp.repeat(heights, extent[axis_at] // blocks).reshape([-1 if axis == axis_at else 1 for axis in range(len(extent))])
    return factor_of


def normal_values(own_key, extent, deviation, bound, shards=(), held_as=jnp.bfloat16):
    result = deviation * jax.random.normal(own_key, extent, jnp.float32)
    if shards:
        result = result * block_scale(own_key, extent, shards, -0.22, 0.18)
    return jnp.clip(result, -bound, bound).astype(held_as)


def setup_inputs(seed: int = 0) -> dict:
    key_of = jax.random.split(jax.random.key(seed), 5)
    state = normal_values(key_of[0], (ROWS, 2 * HARM + 1, VARS, CJ, NT), 1.0, 6.0, ((0, 2), (4, 16)), jnp.float32)
    inflow = normal_values(key_of[1], (2 * HARM + 1, VARS, NT), 1.0, 6.0, ((2, 16),), jnp.float32)
    blade_counts = jax.random.randint(key_of[2], (ROWS,), 20, 61).astype(jnp.int32)
    modes = with_ends(jax.random.randint(key_of[3], (IFACES, HARM), 1, 41), jax.random.fold_in(key_of[3], 1), 1, 40).astype(jnp.int32)
    return dict(state=state, inflow=inflow, blade_counts=blade_counts, modes=modes)


DIFFUSE = 0.05
FOURTH_SMOOTH = 0.03
COURANT = 0.6
FREQ_SCALE = 0.02
SECTION_WEIGHTS = (0.5, 1.0)


def residual(padded, frequency):
    inner_depth = padded.shape[2] - 4
    inner_width = padded.shape[3] - 4

    def window_at(source, shift_j, shift_t):
        return source[:, :, 2 + shift_j:2 + shift_j + inner_depth, 2 + shift_t:2 + shift_t + inner_width]

    steady = padded[0]
    speed_axial = 1.0 + 0.5 * jnp.tanh(steady[1])
    speed_turn = 0.5 * jnp.tanh(steady[2])
    cosines = padded[1::2]
    sines = padded[2::2]
    stress = 0.5 * jnp.sum(cosines[:, 1:2] * cosines + sines[:, 1:2] * sines, axis=0)
    flux_axial = speed_axial * padded + jnp.concatenate([stress[None], jnp.zeros_like(padded[1:])], axis=0)
    flux_turn = speed_turn * padded
    center = window_at(padded, 0, 0)
    neighbours = window_at(padded, 1, 0) + window_at(padded, -1, 0) + window_at(padded, 0, 1) + window_at(padded, 0, -1)
    farther = window_at(padded, 2, 0) + window_at(padded, -2, 0) + window_at(padded, 0, 2) + window_at(padded, 0, -2)
    convect = -0.5 * (window_at(flux_axial, 1, 0) - window_at(flux_axial, -1, 0)) - 0.5 * (window_at(flux_turn, 0, 1) - window_at(flux_turn, 0, -1))
    second = neighbours - 4.0 * center
    fourth = farther - 4.0 * neighbours + 12.0 * center
    rates = frequency[:, None, None, None]
    source_real = rates * center[2::2]
    source_imag = -rates * center[1::2]
    paired = jnp.stack([source_real, source_imag], axis=1).reshape((-1,) + center.shape[1:])
    source = jnp.concatenate([jnp.zeros_like(center[0:1]), paired], axis=0)
    return convect + DIFFUSE * second - FOURTH_SMOOTH * fourth + source


def local_step(field):
    steady = field[0]
    return COURANT / (1.0 + 0.5 * jnp.tanh(steady[1]) + jnp.abs(0.5 * jnp.tanh(steady[2])))


def rotate_modes(planes, table, sign, columns, total):
    pieces = [planes[0]]
    for harmonic in range(planes.shape[0] // 2):
        turns = jnp.remainder(table[harmonic] * columns, total)
        angle = (2.0 * math.pi / total) * turns.astype(jnp.float32)
        cosine = jnp.cos(angle)
        sine = sign * jnp.sin(angle)
        real_part = planes[1 + 2 * harmonic]
        imag_part = planes[2 + 2 * harmonic]
        pieces.append(real_part * cosine - imag_part * sine)
        pieces.append(real_part * sine + imag_part * cosine)
    return jnp.stack(pieces)


def pad_columns(planes):
    return jnp.pad(planes, ((0, 0), (0, 0), (0, 0), (2, 2)))


def reference(state, inflow, blade_counts, modes):
    columns = jnp.arange(NT, dtype=jnp.int32)
    orders = jnp.arange(1, HARM + 1, dtype=jnp.float32)

    def row_residual(current, row_number, frequency):
        core = current[row_number]
        if row_number == 0:
            lower = jnp.concatenate([inflow[:, :, None, :], inflow[:, :, None, :]], axis=2)
        else:
            lower = rotate_modes(current[row_number - 1][:, :, CJ - 2:], modes[row_number - 1], 1.0, columns, NT)
        if row_number == ROWS - 1:
            last_plane = core[:, :, CJ - 1:]
            upper = jnp.concatenate([last_plane, last_plane], axis=2)
        else:
            upper = rotate_modes(current[row_number + 1][:, :, :2], modes[row_number], -1.0, columns, NT)
        wrapped = jnp.concatenate([core[..., NT - 2:], core, core[..., :2]], axis=3)
        padded = jnp.concatenate([pad_columns(lower), wrapped, pad_columns(upper)], axis=2)

        def block_residual(block_number):
            piece = lax.dynamic_slice_in_dim(padded, block_number * CT, CT + 4, 3)
            return residual(piece, frequency)

        blocks = lax.map(block_residual, jnp.arange(N_BLK, dtype=jnp.int32))
        return jnp.moveaxis(blocks, 0, 3).reshape((2 * HARM + 1, VARS, CJ, NT))

    step_sizes = [local_step(state[row_number]) for row_number in range(ROWS)]
    frequencies = [FREQ_SCALE * blade_counts[row_number].astype(jnp.float32) * orders for row_number in range(ROWS)]
    current = state
    for weight in SECTION_WEIGHTS:
        current = jnp.stack([state[row_number] + weight * step_sizes[row_number] * row_residual(current, row_number, frequencies[row_number]) for row_number in range(ROWS)])
    return current
```

```python
import functools
import math

import jax
import jax.numpy as jnp
from jax import lax
from jax.experimental import pallas as pl
from jax.experimental.pallas import tpu as pltpu
from jax.sharding import PartitionSpec as P

DIFFUSE = 0.05
FOURTH_SMOOTH = 0.03
COURANT = 0.6
FREQ_SCALE = 0.02
MESH = pl.DeviceIdType.MESH
NEAR = DIFFUSE + 4.0 * FOURTH_SMOOTH
CENTER = -4.0 * DIFFUSE - 12.0 * FOURTH_SMOOTH
HALO = 4
PAD = 8


def section(src, base, rows, start, start_base, weight, rates, emit, comps, nvars):
    width = src.shape[2]

    def at(c, v, off):
        return src[c * nvars + v, base + off : base + off + rows, :]

    def opening(v):
        return start[v, start_base : start_base + rows, :]

    coef_up = (NEAR - 0.5) - 0.25 * jnp.tanh(at(0, 1, 1))
    coef_down = (NEAR + 0.5) + 0.25 * jnp.tanh(at(0, 1, -1))
    half_turn = 0.25 * jnp.tanh(at(0, 2, 0))
    coef_next = NEAR - pltpu.roll(half_turn, width - 1, 1)
    coef_prev = NEAR + pltpu.roll(half_turn, 1, 1)
    step = (weight * COURANT) / (
        1.0 + 0.5 * jnp.tanh(opening(1)) + jnp.abs(0.5 * jnp.tanh(opening(2)))
    )

    def one(c, v):
        here, up, down = at(c, v, 0), at(c, v, 1), at(c, v, -1)
        far = (
            at(c, v, 2)
            + at(c, v, -2)
            + pltpu.roll(here, width - 2, 1)
            + pltpu.roll(here, 2, 1)
        )
        total = (
            coef_up * up
            + coef_down * down
            + coef_next * pltpu.roll(here, width - 1, 1)
            + coef_prev * pltpu.roll(here, 1, 1)
            + CENTER * here
            - FOURTH_SMOOTH * far
        )
        return here, up, down, total

    def put(c, v, total):
        k = c * nvars + v
        emit(k, start[k, start_base : start_base + rows, :] + step * total)

    def per_var(v, carry):
        stress = None
        for n in range(1, comps // 2 + 1):
            real, real_up, real_down, real_total = one(2 * n - 1, v)
            imag, imag_up, imag_down, imag_total = one(2 * n, v)
            rate = rates[n - 1]
            put(2 * n - 1, v, real_total + rate * imag)
            put(2 * n, v, imag_total - rate * real)
            term = (
                at(2 * n - 1, 1, 1) * real_up
                + at(2 * n, 1, 1) * imag_up
                - at(2 * n - 1, 1, -1) * real_down
                - at(2 * n, 1, -1) * imag_down
            )
            stress = term if stress is None else stress + term
        _, _, _, total = one(0, v)
        put(0, v, total - 0.25 * stress)
        return carry

    lax.fori_loop(0, nvars, per_var, 0)


def kernel(
    rows_total,
    blocks,
    nvars,
    modes,
    counts,
    state,
    inflow,
    out,
    e_main,
    e_edge,
    f_main,
    f_edge,
    x_main,
    x_edge,
    y_main,
    y_edge,
    in_main,
    in_edge,
    pack,
    halo,
    low,
    high,
    low_halo,
    high_halo,
    local_sem,
    send_sem,
    recv_sem,
):
    fields, depth, width = state.shape
    comps = fields // nvars
    harmonics = comps // 2
    slots = width // HALO
    groups = -(-fields // slots)
    layers = depth // 8
    total_columns = width * blocks
    row = lax.axis_index("row")
    blk = lax.axis_index("blk")
    right = lax.rem(blk + 1, blocks)
    left = lax.rem(blk + blocks - 1, blocks)
    has_low = row > 0
    has_high = row < rows_total - 1

    barrier = pltpu.get_barrier_semaphore()

    def greet(r, b):
        pl.semaphore_signal(barrier, inc=1, device_id={"row": r, "blk": b}, device_id_type=MESH)

    greet(row, right)
    greet(row, left)

    @pl.when(has_high)
    def _():
        greet(row + 1, right)
        greet(row + 1, left)
        greet(row + 1, blk)

    @pl.when(has_low)
    def _():
        greet(row - 1, right)
        greet(row - 1, left)
        greet(row - 1, blk)

    fetch = pltpu.make_async_copy(state, e_main.at[:, PAD : PAD + depth, :], local_sem.at[0])
    fetch_in = pltpu.make_async_copy(inflow, in_main, local_sem.at[1])
    fetch.start()
    fetch_in.start()

    shape = (8, width)
    sub = lax.broadcasted_iota(jnp.int32, shape, 0)
    lane = lax.broadcasted_iota(jnp.int32, shape, 1)
    sign = jnp.where((sub // 2) % 2 == 0, 1.0, -1.0).astype(jnp.float32)

    def mode_of(interface, n):
        value = jnp.int32(0)
        for i in range(rows_total - 1):
            value = value + jnp.where(interface == i, modes[i, n], 0)
        return value

    def count_of(wanted):
        value = jnp.int32(0)
        for i in range(rows_total):
            value = value + jnp.where(wanted == i, counts[i], 0)
        return value.astype(jnp.float32)

    def tables(columns):
        made = []
        for n in range(harmonics):
            mode = jnp.where(sub < 4, mode_of(row - 1, n), mode_of(row, n))
            product = mode * columns
            if total_columns & (total_columns - 1) == 0:
                turns = product & (total_columns - 1)
            else:
                turns = jnp.remainder(product, total_columns)
            angle = (2.0 * math.pi / total_columns) * turns.astype(jnp.float32)
            made.append((jnp.cos(angle), sign * jnp.sin(angle)))
        return made

    tab_main = tables(blk * width + lane)
    tab_edge = tables(blk * width + jnp.where(lane < width // 2, lane - HALO, lane + HALO))
    own_rate = FREQ_SCALE * count_of(row)
    next_rate = jnp.where(sub < 4, FREQ_SCALE * count_of(row - 1), FREQ_SCALE * count_of(row + 1))
    own_rates = [own_rate * float(n) for n in range(1, harmonics + 1)]
    next_rates = [next_rate * float(n) for n in range(1, harmonics + 1)]

    fetch.wait()
    fetch_in.wait()

    def widen(value):
        at_lane = lax.broadcasted_iota(jnp.int32, value.shape, 1)
        return jnp.where(
            at_lane < width // 2,
            pltpu.roll(value, HALO, 1),
            pltpu.roll(value, width - HALO, 1),
        )

    for layer in range(layers):
        for g in range(groups):
            left_edge = jnp.zeros(shape, jnp.float32)
            right_edge = jnp.zeros(shape, jnp.float32)
            for m in range(min(slots, fields - g * slots)):
                start_row = PAD + 8 * layer
                value = e_main[g * slots + m, start_row : start_row + 8, :]
                spot = lane // HALO == m
                left_edge = jnp.where(spot, pltpu.roll(value, HALO * m, 1), left_edge)
                right_edge = jnp.where(
                    spot, pltpu.roll(value, (HALO * m + HALO) % width, 1), right_edge
                )
            pack[0, layer * groups + g] = left_edge
            pack[1, layer * groups + g] = right_edge
    left_edge = jnp.zeros((nvars, width), jnp.float32)
    right_edge = jnp.zeros((nvars, width), jnp.float32)
    lane_in = lax.broadcasted_iota(jnp.int32, (nvars, width), 1)
    for c in range(comps):
        value = in_main[c]
        spot = lane_in // HALO == c
        left_edge = jnp.where(spot, pltpu.roll(value, HALO * c, 1), left_edge)
        right_edge = jnp.where(spot, pltpu.roll(value, (HALO * c + HALO) % width, 1), right_edge)
        in_edge[c] = widen(value)
    pack[0, layers * groups, 0:nvars, :] = left_edge
    pack[1, layers * groups, 0:nvars, :] = right_edge

    greeters = 2 + 3 * has_low.astype(jnp.int32) + 3 * has_high.astype(jnp.int32)
    pl.semaphore_wait(barrier, greeters)

    def send(src, dst, index, r, b):
        return pltpu.make_async_remote_copy(
            src_ref=src,
            dst_ref=dst,
            send_sem=send_sem.at[index],
            recv_sem=recv_sem.at[index],
            device_id={"row": r, "blk": b},
            device_id_type=MESH,
        )

    bottom = pl.ds(0, groups)
    top = pl.ds((layers - 1) * groups, groups)
    level = [send(pack.at[1], halo.at[0], 0, row, right), send(pack.at[0], halo.at[1], 1, row, left)]
    up = [
        send(pack.at[1, top], low_halo.at[0], 2, row + 1, right),
        send(pack.at[0, top], low_halo.at[1], 3, row + 1, left),
        send(state.at[:, pl.ds(depth - 8, 8), :], low, 4, row + 1, blk),
    ]
    down = [
        send(pack.at[1, bottom], high_halo.at[0], 5, row - 1, right),
        send(pack.at[0, bottom], high_halo.at[1], 6, row - 1, left),
        send(state.at[:, pl.ds(0, 8), :], high, 7, row - 1, blk),
    ]
    for copy in level:
        copy.start()

    @pl.when(has_high)
    def _():
        for copy in up:
            copy.start()

    @pl.when(has_low)
    def _():
        for copy in down:
            copy.start()

    for k in range(fields):
        e_edge[k, PAD : PAD + depth, :] = widen(e_main[k, PAD : PAD + depth, :])

    @pl.when(has_low)
    def _():
        up[2].wait_recv()
        x_main[:, 0:4, :] = low[:, 4:8, :]

    @pl.when(jnp.logical_not(has_low))
    def _():
        x_main[:, 0:4, :] = jnp.zeros((fields, 4, width), jnp.float32)

    @pl.when(has_high)
    def _():
        down[2].wait_recv()
        x_main[:, 8:12, :] = high[:, 0:4, :]

    @pl.when(jnp.logical_not(has_high))
    def _():
        x_main[:, 8:12, :] = jnp.zeros((fields, 4, width), jnp.float32)

    def ends(field, inflow_of):
        @pl.when(jnp.logical_not(has_low))
        def _():
            for c in range(comps):
                for v in range(nvars):
                    plane = inflow_of[c, v : v + 1, :]
                    field[c * nvars + v, PAD - 2 : PAD, :] = jnp.broadcast_to(plane, (2, width))

        @pl.when(jnp.logical_not(has_high))
        def _():
            for k in range(fields):
                plane = field[k, PAD + depth - 1 : PAD + depth, :]
                field[k, PAD + depth : PAD + depth + 2, :] = jnp.broadcast_to(plane, (2, width))

    def turn(load, save, table):
        def per_var(v, carry):
            save(v, load(v))
            for n in range(harmonics):
                cosine, sine = table[n]
                real_at, imag_at = (2 * n + 1) * nvars + v, (2 * n + 2) * nvars + v
                real, imag = load(real_at), load(imag_at)
                save(real_at, real * cosine - imag * sine)
                save(imag_at, real * sine + imag * cosine)
            return carry

        lax.fori_loop(0, nvars, per_var, 0)

    def both(e, f, x, y, inflow_of, table, emit):
        x[:, 4:6, :] = e[:, PAD : PAD + 2, :]
        x[:, 6:8, :] = e[:, PAD + depth - 2 : PAD + depth, :]

        def save_first(k, value):
            e[k, PAD - 2 : PAD, :] = value[0:2]
            x[k, 4:8, :] = value[2:6]
            e[k, PAD + depth : PAD + depth + 2, :] = value[6:8]

        turn(lambda k: x[k, 2:10, :], save_first, table)
        ends(e, inflow_of)

        def keep_y(k, value):
            y[k] = value

        def keep_f(k, value):
            f[k, PAD : PAD + depth, :] = value

        section(x, 2, 8, x, 2, 0.5, next_rates, keep_y, comps, nvars)
        section(e, PAD, depth, e, PAD, 0.5, own_rates, keep_f, comps, nvars)

        def save_second(k, value):
            f[k, PAD - 2 : PAD, :] = value[0:2]
            f[k, PAD + depth : PAD + depth + 2, :] = value[6:8]

        turn(lambda k: y[k], save_second, table)
        ends(f, inflow_of)
        section(f, PAD, depth, e, PAD, 1.0, own_rates, emit, comps, nvars)

    def emit_main(k, value):
        out[k] = value

    both(e_main, f_main, x_main, y_main, in_main, tab_main, emit_main)

    for k in range(fields):
        x_edge[k, 0:8, :] = widen(x_main[k, 0:8, :])
        x_edge[k, 8:16, :] = widen(x_main[k, 8:16, :])

    for copy in level:
        copy.wait_recv()

    def mended(value, from_left, from_right, m):
        at_lane = lax.broadcasted_iota(jnp.int32, value.shape, 1)
        left_part = pltpu.roll(from_left, (width - HALO * m) % width, 1)
        right_part = pltpu.roll(from_right, (2 * width - HALO - HALO * m) % width, 1)
        return jnp.where(
            at_lane < HALO, left_part, jnp.where(at_lane >= width - HALO, right_part, value)
        )

    for layer in range(layers):
        for k in range(fields):
            g, m = k // slots, k % slots
            spot = slice(PAD + 8 * layer, PAD + 8 * layer + 8)
            at = layer * groups + g
            e_edge[k, spot, :] = mended(e_edge[k, spot, :], halo[0, at], halo[1, at], m)
    for c in range(comps):
        at = layers * groups
        in_edge[c] = mended(in_edge[c], halo[0, at, 0:nvars, :], halo[1, at, 0:nvars, :], c)

    @pl.when(has_low)
    def _():
        up[0].wait_recv()
        up[1].wait_recv()
        for k in range(fields):
            g, m = k // slots, k % slots
            x_edge[k, 0:4, :] = mended(
                x_edge[k, 0:4, :], low_halo[0, g, 4:8, :], low_halo[1, g, 4:8, :], m
            )

    @pl.when(has_high)
    def _():
        down[0].wait_recv()
        down[1].wait_recv()
        for k in range(fields):
            g, m = k // slots, k % slots
            x_edge[k, 8:12, :] = mended(
                x_edge[k, 8:12, :], high_halo[0, g, 0:4, :], high_halo[1, g, 0:4, :], m
            )

    def emit_edge(k, value):
        at_lane = lax.broadcasted_iota(jnp.int32, value.shape, 1)
        first = at_lane < HALO
        last = at_lane >= width - HALO
        moved = jnp.where(first, pltpu.roll(value, width - HALO, 1), pltpu.roll(value, HALO, 1))
        out[k] = jnp.where(jnp.logical_or(first, last), moved, out[k])

    both(e_edge, f_edge, x_edge, y_edge, in_edge, tab_edge, emit_edge)

    for copy in level:
        copy.wait_send()

    @pl.when(has_high)
    def _():
        for copy in up:
            copy.wait_send()

    @pl.when(has_low)
    def _():
        for copy in down:
            copy.wait_send()


def body(rows_total, blocks, state, inflow, blade_counts, modes):
    _, comps, nvars, depth, width = state.shape
    fields = comps * nvars
    groups = -(-fields // (width // HALO))
    layers = depth // 8
    f32 = jnp.float32

    def buf(*shape):
        return pltpu.VMEM(shape, f32)

    tall = depth + 2 * PAD
    result = pl.pallas_call(
        functools.partial(kernel, rows_total, blocks, nvars),
        out_shape=jax.ShapeDtypeStruct((fields, depth, width), f32),
        in_specs=[
            pl.BlockSpec(memory_space=pltpu.SMEM),
            pl.BlockSpec(memory_space=pltpu.SMEM),
            pl.BlockSpec(memory_space=pl.ANY),
            pl.BlockSpec(memory_space=pl.ANY),
        ],
        out_specs=pl.BlockSpec(memory_space=pltpu.VMEM),
        scratch_shapes=[
            buf(fields, tall, width),
            buf(fields, tall, width),
            buf(fields, tall, width),
            buf(fields, tall, width),
            buf(fields, 16, width),
            buf(fields, 16, width),
            buf(fields, 8, width),
            buf(fields, 8, width),
            buf(comps, nvars, width),
            buf(comps, nvars, width),
            buf(2, layers * groups + 1, 8, width),
            buf(2, layers * groups + 1, 8, width),
            buf(fields, 8, width),
            buf(fields, 8, width),
            buf(2, groups, 8, width),
            buf(2, groups, 8, width),
            pltpu.SemaphoreType.DMA((2,)),
            pltpu.SemaphoreType.DMA((8,)),
            pltpu.SemaphoreType.DMA((8,)),
        ],
        compiler_params=pltpu.CompilerParams(collective_id=0, has_side_effects=True),
    )(modes, blade_counts, state.reshape(fields, depth, width), inflow)
    return result.reshape(1, comps, nvars, depth, width)


def solution(mesh):
    placed = (P("row", None, None, None, "blk"), P(None, None, "blk"), P(), P())
    return jax.shard_map(
        functools.partial(body, mesh.shape["row"], mesh.shape["blk"]),
        mesh=mesh,
        in_specs=placed,
        out_specs=P("row", None, None, None, "blk"),
        check_vma=False,
    )
```

```python
import functools
import math

import jax
import jax.numpy as jnp
from jax import lax
from jax.experimental import pallas as pl
from jax.experimental.pallas import tpu as pltpu
from jax.sharding import PartitionSpec as P

DIFFUSE = 0.05
FOURTH_SMOOTH = 0.03
COURANT = 0.6
FREQ_SCALE = 0.02
MESH = pl.DeviceIdType.MESH
NEAR = DIFFUSE + 4.0 * FOURTH_SMOOTH
CENTER = -4.0 * DIFFUSE - 12.0 * FOURTH_SMOOTH
HALO = 4
PAD = 8


def section(src, base, rows, start, start_base, weight, rates, emit, comps, nvars):
    width = src.shape[2]

    def at(c, v, off):
        return src[c * nvars + v, base + off : base + off + rows, :]

    def opening(v):
        return start[v, start_base : start_base + rows, :]

    coef_up = (NEAR - 0.5) - 0.25 * jnp.tanh(at(0, 1, 1))
    coef_down = (NEAR + 0.5) + 0.25 * jnp.tanh(at(0, 1, -1))
    half_turn = 0.25 * jnp.tanh(at(0, 2, 0))
    coef_next = NEAR - pltpu.roll(half_turn, width - 1, 1)
    coef_prev = NEAR + pltpu.roll(half_turn, 1, 1)
    step = (weight * COURANT) / (
        1.0 + 0.5 * jnp.tanh(opening(1)) + jnp.abs(0.5 * jnp.tanh(opening(2)))
    )

    def one(c, v):
        here, up, down = at(c, v, 0), at(c, v, 1), at(c, v, -1)
        far = (
            at(c, v, 2)
            + at(c, v, -2)
            + pltpu.roll(here, width - 2, 1)
            + pltpu.roll(here, 2, 1)
        )
        total = (
            coef_up * up
            + coef_down * down
            + coef_next * pltpu.roll(here, width - 1, 1)
            + coef_prev * pltpu.roll(here, 1, 1)
            + CENTER * here
            - FOURTH_SMOOTH * far
        )
        return here, up, down, total

    def put(c, v, total):
        k = c * nvars + v
        emit(k, start[k, start_base : start_base + rows, :] + step * total)

    def per_var(v, carry):
        stress = None
        for n in range(1, comps // 2 + 1):
            real, real_up, real_down, real_total = one(2 * n - 1, v)
            imag, imag_up, imag_down, imag_total = one(2 * n, v)
            rate = rates[n - 1]
            put(2 * n - 1, v, real_total + rate * imag)
            put(2 * n, v, imag_total - rate * real)
            term = (
                at(2 * n - 1, 1, 1) * real_up
                + at(2 * n, 1, 1) * imag_up
                - at(2 * n - 1, 1, -1) * real_down
                - at(2 * n, 1, -1) * imag_down
            )
            stress = term if stress is None else stress + term
        _, _, _, total = one(0, v)
        put(0, v, total - 0.25 * stress)
        return carry

    lax.fori_loop(0, nvars, per_var, 0)


def kernel(
    rows_total,
    blocks,
    nvars,
    modes_in,
    counts_in,
    state,
    inflow,
    out,
    e_main,
    e_edge,
    f_main,
    f_edge,
    x_main,
    x_edge,
    y_main,
    y_edge,
    in_main,
    in_edge,
    pack,
    corner,
    halo,
    low,
    high,
    low_halo,
    high_halo,
    modes,
    counts,
    local_sem,
    send_sem,
    recv_sem,
):
    fields, depth, width = state.shape
    comps = fields // nvars
    harmonics = comps // 2
    slots = width // HALO
    groups = -(-(fields + comps) // slots)
    layers = depth // 8
    total_columns = width * blocks
    row = lax.axis_index("row")
    blk = lax.axis_index("blk")
    right = lax.rem(blk + 1, blocks)
    left = lax.rem(blk + blocks - 1, blocks)
    has_low = row > 0
    has_high = row < rows_total - 1

    barrier = pltpu.get_barrier_semaphore()

    def greet(r, b):
        pl.semaphore_signal(barrier, inc=1, device_id={"row": r, "blk": b}, device_id_type=MESH)

    greet(row, right)
    greet(row, left)

    @pl.when(has_high)
    def _():
        greet(row + 1, right)
        greet(row + 1, left)
        greet(row + 1, blk)

    @pl.when(has_low)
    def _():
        greet(row - 1, right)
        greet(row - 1, left)
        greet(row - 1, blk)

    fetch = pltpu.make_async_copy(state, e_main.at[:, PAD : PAD + depth, :], local_sem.at[0])
    fetch_in = pltpu.make_async_copy(inflow, in_main, local_sem.at[1])
    fetch_modes = pltpu.make_async_copy(modes_in, modes, local_sem.at[2])
    fetch_counts = pltpu.make_async_copy(counts_in, counts, local_sem.at[3])
    for copy in (fetch_modes, fetch_counts, fetch, fetch_in):
        copy.start()
    fetch_modes.wait()
    fetch_counts.wait()

    shape = (8, width)
    sub = lax.broadcasted_iota(jnp.int32, shape, 0)
    lane = lax.broadcasted_iota(jnp.int32, shape, 1)
    sign = jnp.where((sub // 2) % 2 == 0, 1.0, -1.0).astype(jnp.float32)

    def mode_of(interface, n):
        value = jnp.int32(0)
        for i in range(rows_total - 1):
            value = value + jnp.where(interface == i, modes[i, n], 0)
        return value

    def count_of(wanted):
        value = jnp.int32(0)
        for i in range(rows_total):
            value = value + jnp.where(wanted == i, counts[i], 0)
        return value.astype(jnp.float32)

    def tables(columns):
        made = []
        for n in range(harmonics):
            mode = jnp.where(sub < 4, mode_of(row - 1, n), mode_of(row, n))
            product = mode * columns
            if total_columns & (total_columns - 1) == 0:
                turns = product & (total_columns - 1)
            else:
                turns = jnp.remainder(product, total_columns)
            angle = (2.0 * math.pi / total_columns) * turns.astype(jnp.float32)
            made.append((jnp.cos(angle), sign * jnp.sin(angle)))
        return made

    tab_main = tables(blk * width + lane)
    tab_edge = tables(blk * width + jnp.where(lane < width // 2, lane - HALO, lane + HALO))
    own_rate = FREQ_SCALE * count_of(row)
    next_rate = jnp.where(sub < 4, FREQ_SCALE * count_of(row - 1), FREQ_SCALE * count_of(row + 1))
    own_rates = [own_rate * float(n) for n in range(1, harmonics + 1)]
    next_rates = [next_rate * float(n) for n in range(1, harmonics + 1)]

    fetch.wait()
    fetch_in.wait()

    def widen(value):
        at_lane = lax.broadcasted_iota(jnp.int32, value.shape, 1)
        return jnp.where(
            at_lane < width // 2,
            pltpu.roll(value, HALO, 1),
            pltpu.roll(value, width - HALO, 1),
        )

    for layer in range(layers):
        for g in range(groups):
            left_edge = jnp.zeros(shape, jnp.float32)
            right_edge = jnp.zeros(shape, jnp.float32)
            for m in range(max(0, min(slots, fields - g * slots))):
                start_row = PAD + 8 * layer
                value = e_main[g * slots + m, start_row : start_row + 8, :]
                spot = lane // HALO == m
                left_edge = jnp.where(spot, pltpu.roll(value, HALO * m, 1), left_edge)
                right_edge = jnp.where(
                    spot, pltpu.roll(value, (HALO * m + HALO) % width, 1), right_edge
                )
            pack[0, layer * groups + g] = left_edge
            pack[1, layer * groups + g] = right_edge
    lane_in = lax.broadcasted_iota(jnp.int32, (nvars, width), 1)
    for g in range(fields // slots, groups):
        left_edge = pack[0, g, 0:nvars, :]
        right_edge = pack[1, g, 0:nvars, :]
        for c in range(comps):
            m = fields + c - g * slots
            if 0 <= m < slots:
                value = in_main[c]
                spot = lane_in // HALO == m
                left_edge = jnp.where(spot, pltpu.roll(value, HALO * m, 1), left_edge)
                right_edge = jnp.where(
                    spot, pltpu.roll(value, (HALO * m + HALO) % width, 1), right_edge
                )
        pack[0, g, 0:nvars, :] = left_edge
        pack[1, g, 0:nvars, :] = right_edge
    for c in range(comps):
        in_edge[c] = widen(in_main[c])
    for side in range(2):
        for g in range(groups):
            corner[0, side, 2 * g : 2 * g + 2, :] = pack[side, g, 0:2, :]
            corner[1, side, 2 * g : 2 * g + 2, :] = pack[side, (layers - 1) * groups + g, 6:8, :]

    greeters = 2 + 3 * has_low.astype(jnp.int32) + 3 * has_high.astype(jnp.int32)
    pl.semaphore_wait(barrier, greeters)

    def send(src, dst, index, r, b):
        return pltpu.make_async_remote_copy(
            src_ref=src,
            dst_ref=dst,
            send_sem=send_sem.at[index],
            recv_sem=recv_sem.at[index],
            device_id={"row": r, "blk": b},
            device_id_type=MESH,
        )

    level = [send(pack.at[1], halo.at[0], 0, row, right), send(pack.at[0], halo.at[1], 1, row, left)]
    up = [
        send(corner.at[1, 1], low_halo.at[0], 2, row + 1, right),
        send(corner.at[1, 0], low_halo.at[1], 3, row + 1, left),
        send(state.at[:, pl.ds(depth - 8, 8), :], low, 4, row + 1, blk),
    ]
    down = [
        send(corner.at[0, 1], high_halo.at[0], 5, row - 1, right),
        send(corner.at[0, 0], high_halo.at[1], 6, row - 1, left),
        send(state.at[:, pl.ds(0, 8), :], high, 7, row - 1, blk),
    ]
    for copy in level:
        copy.start()

    @pl.when(has_high)
    def _():
        for copy in up:
            copy.start()

    @pl.when(has_low)
    def _():
        for copy in down:
            copy.start()

    for k in range(fields):
        e_edge[k, PAD : PAD + depth, :] = widen(e_main[k, PAD : PAD + depth, :])

    @pl.when(has_low)
    def _():
        up[2].wait_recv()
        x_main[:, 0:4, :] = low[:, 4:8, :]

    @pl.when(jnp.logical_not(has_low))
    def _():
        x_main[:, 0:4, :] = jnp.zeros((fields, 4, width), jnp.float32)

    @pl.when(has_high)
    def _():
        down[2].wait_recv()
        x_main[:, 8:12, :] = high[:, 0:4, :]

    @pl.when(jnp.logical_not(has_high))
    def _():
        x_main[:, 8:12, :] = jnp.zeros((fields, 4, width), jnp.float32)

    def ends(field, inflow_of):
        @pl.when(jnp.logical_not(has_low))
        def _():
            for c in range(comps):
                for v in range(nvars):
                    plane = inflow_of[c, v : v + 1, :]
                    field[c * nvars + v, PAD - 2 : PAD, :] = jnp.broadcast_to(plane, (2, width))

        @pl.when(jnp.logical_not(has_high))
        def _():
            for k in range(fields):
                plane = field[k, PAD + depth - 1 : PAD + depth, :]
                field[k, PAD + depth : PAD + depth + 2, :] = jnp.broadcast_to(plane, (2, width))

    def turn(load, save, table):
        def per_var(v, carry):
            save(v, load(v))
            for n in range(harmonics):
                cosine, sine = table[n]
                real_at, imag_at = (2 * n + 1) * nvars + v, (2 * n + 2) * nvars + v
                real, imag = load(real_at), load(imag_at)
                save(real_at, real * cosine - imag * sine)
                save(imag_at, real * sine + imag * cosine)
            return carry

        lax.fori_loop(0, nvars, per_var, 0)

    def both(e, f, x, y, inflow_of, table, emit):
        x[:, 4:6, :] = e[:, PAD : PAD + 2, :]
        x[:, 6:8, :] = e[:, PAD + depth - 2 : PAD + depth, :]

        def save_first(k, value):
            e[k, PAD - 2 : PAD, :] = value[0:2]
            x[k, 4:8, :] = value[2:6]
            e[k, PAD + depth : PAD + depth + 2, :] = value[6:8]

        turn(lambda k: x[k, 2:10, :], save_first, table)
        ends(e, inflow_of)

        def keep_y(k, value):
            y[k] = value

        def keep_f(k, value):
            f[k, PAD : PAD + depth, :] = value

        section(x, 2, 8, x, 2, 0.5, next_rates, keep_y, comps, nvars)
        section(e, PAD, depth, e, PAD, 0.5, own_rates, keep_f, comps, nvars)

        def save_second(k, value):
            f[k, PAD - 2 : PAD, :] = value[0:2]
            f[k, PAD + depth : PAD + depth + 2, :] = value[6:8]

        turn(lambda k: y[k], save_second, table)
        ends(f, inflow_of)
        section(f, PAD, depth, e, PAD, 1.0, own_rates, emit, comps, nvars)

    def emit_main(k, value):
        out[k] = value

    both(e_main, f_main, x_main, y_main, in_main, tab_main, emit_main)

    for k in range(fields):
        x_edge[k, 0:8, :] = widen(x_main[k, 0:8, :])
        x_edge[k, 8:16, :] = widen(x_main[k, 8:16, :])

    for copy in level:
        copy.wait_recv()

    def mended(value, from_left, from_right, m):
        at_lane = lax.broadcasted_iota(jnp.int32, value.shape, 1)
        left_part = pltpu.roll(from_left, (width - HALO * m) % width, 1)
        right_part = pltpu.roll(from_right, (2 * width - HALO - HALO * m) % width, 1)
        return jnp.where(
            at_lane < HALO, left_part, jnp.where(at_lane >= width - HALO, right_part, value)
        )

    for layer in range(layers):
        for k in range(fields):
            g, m = k // slots, k % slots
            spot = slice(PAD + 8 * layer, PAD + 8 * layer + 8)
            at = layer * groups + g
            e_edge[k, spot, :] = mended(e_edge[k, spot, :], halo[0, at], halo[1, at], m)
    for c in range(comps):
        g, m = (fields + c) // slots, (fields + c) % slots
        in_edge[c] = mended(in_edge[c], halo[0, g, 0:nvars, :], halo[1, g, 0:nvars, :], m)

    @pl.when(has_low)
    def _():
        up[0].wait_recv()
        up[1].wait_recv()
        for k in range(fields):
            g, m = k // slots, k % slots
            spot = slice(2 * g, 2 * g + 2)
            x_edge[k, 2:4, :] = mended(
                x_edge[k, 2:4, :], low_halo[0, spot, :], low_halo[1, spot, :], m
            )

    @pl.when(has_high)
    def _():
        down[0].wait_recv()
        down[1].wait_recv()
        for k in range(fields):
            g, m = k // slots, k % slots
            spot = slice(2 * g, 2 * g + 2)
            x_edge[k, 8:10, :] = mended(
                x_edge[k, 8:10, :], high_halo[0, spot, :], high_halo[1, spot, :], m
            )

    def emit_edge(k, value):
        at_lane = lax.broadcasted_iota(jnp.int32, value.shape, 1)
        first = at_lane < HALO
        last = at_lane >= width - HALO
        moved = jnp.where(first, pltpu.roll(value, width - HALO, 1), pltpu.roll(value, HALO, 1))
        out[k] = jnp.where(jnp.logical_or(first, last), moved, out[k])

    both(e_edge, f_edge, x_edge, y_edge, in_edge, tab_edge, emit_edge)

    for copy in level:
        copy.wait_send()

    @pl.when(has_high)
    def _():
        for copy in up:
            copy.wait_send()

    @pl.when(has_low)
    def _():
        for copy in down:
            copy.wait_send()


def body(rows_total, blocks, state, inflow, blade_counts, modes):
    _, comps, nvars, depth, width = state.shape
    fields = comps * nvars
    groups = -(-(fields + comps) // (width // HALO))
    corner_rows = -(-2 * groups // 8) * 8
    layers = depth // 8
    f32 = jnp.float32

    def buf(*shape):
        return pltpu.VMEM(shape, f32)

    tall = depth + 2 * PAD
    result = pl.pallas_call(
        functools.partial(kernel, rows_total, blocks, nvars),
        out_shape=jax.ShapeDtypeStruct((fields, depth, width), f32),
        in_specs=[
            pl.BlockSpec(memory_space=pltpu.HBM),
            pl.BlockSpec(memory_space=pltpu.HBM),
            pl.BlockSpec(memory_space=pltpu.HBM),
            pl.BlockSpec(memory_space=pltpu.HBM),
        ],
        out_specs=pl.BlockSpec(memory_space=pltpu.VMEM),
        scratch_shapes=[
            buf(fields, tall, width),
            buf(fields, tall, width),
            buf(fields, tall, width),
            buf(fields, tall, width),
            buf(fields, 16, width),
            buf(fields, 16, width),
            buf(fields, 8, width),
            buf(fields, 8, width),
            buf(comps, nvars, width),
            buf(comps, nvars, width),
            buf(2, layers * groups, 8, width),
            buf(2, 2, corner_rows, width),
            buf(2, layers * groups, 8, width),
            buf(fields, 8, width),
            buf(fields, 8, width),
            buf(2, corner_rows, width),
            buf(2, corner_rows, width),
            pltpu.SMEM(modes.shape, jnp.int32),
            pltpu.SMEM(blade_counts.shape, jnp.int32),
            pltpu.SemaphoreType.DMA((4,)),
            pltpu.SemaphoreType.DMA((8,)),
            pltpu.SemaphoreType.DMA((8,)),
        ],
        compiler_params=pltpu.CompilerParams(
            collective_id=0, has_side_effects=True, vmem_limit_bytes=16 << 20
        ),
    )(
        *(
            pltpu.with_memory_space_constraint(value, pltpu.HBM)
            for value in (modes, blade_counts, state.reshape(fields, depth, width), inflow)
        )
    )
    return result.reshape(1, comps, nvars, depth, width)


def solution(mesh):
    placed = (P("row", None, None, None, "blk"), P(None, None, "blk"), P(), P())
    return jax.shard_map(
        functools.partial(body, mesh.shape["row"], mesh.shape["blk"]),
        mesh=mesh,
        in_specs=placed,
        out_specs=P("row", None, None, None, "blk"),
        check_vma=False,
    )
```

```python
import functools
import math

import jax
import jax.numpy as jnp
from jax import lax
from jax.experimental import pallas as pl
from jax.experimental.pallas import tpu as pltpu
from jax.sharding import PartitionSpec as P

DIFFUSE = 0.05
FOURTH_SMOOTH = 0.03
COURANT = 0.6
FREQ_SCALE = 0.02
MESH = pl.DeviceIdType.MESH
NEAR = DIFFUSE + 4.0 * FOURTH_SMOOTH
CENTER = -4.0 * DIFFUSE - 12.0 * FOURTH_SMOOTH
HALO = 4
PAD = 8


def packing(items, layers, width):
    seg = width // (layers + 2)
    slots = width // (layers * seg) * (seg // HALO)
    return seg, -(-items // slots)


def section(src, base, rows, start, start_base, weight, rates, emit, comps, nvars):
    width = src.shape[2]

    def at(c, v, off):
        return src[c * nvars + v, base + off : base + off + rows, :]

    def opening(v):
        return start[v, start_base : start_base + rows, :]

    coef_up = (NEAR - 0.5) - 0.25 * jnp.tanh(at(0, 1, 1))
    coef_down = (NEAR + 0.5) + 0.25 * jnp.tanh(at(0, 1, -1))
    half_turn = 0.25 * jnp.tanh(at(0, 2, 0))
    coef_next = NEAR - pltpu.roll(half_turn, width - 1, 1)
    coef_prev = NEAR + pltpu.roll(half_turn, 1, 1)
    step = (weight * COURANT) / (
        1.0 + 0.5 * jnp.tanh(opening(1)) + jnp.abs(0.5 * jnp.tanh(opening(2)))
    )

    def one(c, v):
        here, up, down = at(c, v, 0), at(c, v, 1), at(c, v, -1)
        far = (
            at(c, v, 2)
            + at(c, v, -2)
            + pltpu.roll(here, width - 2, 1)
            + pltpu.roll(here, 2, 1)
        )
        total = (
            coef_up * up
            + coef_down * down
            + coef_next * pltpu.roll(here, width - 1, 1)
            + coef_prev * pltpu.roll(here, 1, 1)
            + CENTER * here
            - FOURTH_SMOOTH * far
        )
        return here, up, down, total

    def put(c, v, total):
        k = c * nvars + v
        emit(k, start[k, start_base : start_base + rows, :] + step * total)

    def per_var(v, carry):
        stress = None
        for n in range(1, comps // 2 + 1):
            real, real_up, real_down, real_total = one(2 * n - 1, v)
            imag, imag_up, imag_down, imag_total = one(2 * n, v)
            rate = rates[n - 1]
            put(2 * n - 1, v, real_total + rate * imag)
            put(2 * n, v, imag_total - rate * real)
            term = (
                at(2 * n - 1, 1, 1) * real_up
                + at(2 * n, 1, 1) * imag_up
                - at(2 * n - 1, 1, -1) * real_down
                - at(2 * n, 1, -1) * imag_down
            )
            stress = term if stress is None else stress + term
        _, _, _, total = one(0, v)
        put(0, v, total - 0.25 * stress)
        return carry

    lax.fori_loop(0, nvars, per_var, 0)


def kernel(
    rows_total,
    blocks,
    nvars,
    modes_in,
    counts_in,
    state,
    inflow,
    out,
    e_main,
    e_edge,
    f_main,
    f_edge,
    x_main,
    y_main,
    in_main,
    in_edge,
    pack,
    corner,
    halo,
    low,
    high,
    low_halo,
    high_halo,
    modes,
    counts,
    local_sem,
    send_sem,
    recv_sem,
):
    fields, depth, width = state.shape
    comps = fields // nvars
    harmonics = comps // 2
    layers = depth // 8
    seg, groups = packing(fields + comps, layers, width)
    per = seg // HALO
    slots = width // (layers * seg) * per
    total_columns = width * blocks
    row = lax.axis_index("row")
    blk = lax.axis_index("blk")
    right = lax.rem(blk + 1, blocks)
    left = lax.rem(blk + blocks - 1, blocks)
    has_low = row > 0
    has_high = row < rows_total - 1

    barrier = pltpu.get_barrier_semaphore()

    def greet(r, b):
        pl.semaphore_signal(barrier, inc=1, device_id={"row": r, "blk": b}, device_id_type=MESH)

    greet(row, right)
    greet(row, left)

    @pl.when(has_high)
    def _():
        greet(row + 1, right)
        greet(row + 1, left)
        greet(row + 1, blk)

    @pl.when(has_low)
    def _():
        greet(row - 1, right)
        greet(row - 1, left)
        greet(row - 1, blk)

    fetch = pltpu.make_async_copy(state, e_main.at[:, PAD : PAD + depth, :], local_sem.at[0])
    fetch_in = pltpu.make_async_copy(inflow, in_main, local_sem.at[1])
    fetch_modes = pltpu.make_async_copy(modes_in, modes, local_sem.at[2])
    fetch_counts = pltpu.make_async_copy(counts_in, counts, local_sem.at[3])
    for copy in (fetch_modes, fetch_counts, fetch, fetch_in):
        copy.start()
    fetch_modes.wait()
    fetch_counts.wait()

    shape = (8, width)
    sub = lax.broadcasted_iota(jnp.int32, shape, 0)
    lane = lax.broadcasted_iota(jnp.int32, shape, 1)
    sign = jnp.where((sub // 2) % 2 == 0, 1.0, -1.0).astype(jnp.float32)

    def mode_of(interface, n):
        value = jnp.int32(0)
        for i in range(rows_total - 1):
            value = value + jnp.where(interface == i, modes[i, n], 0)
        return value

    def count_of(wanted):
        value = jnp.int32(0)
        for i in range(rows_total):
            value = value + jnp.where(wanted == i, counts[i], 0)
        return value.astype(jnp.float32)

    def tables(modes_at, columns):
        made = []
        for n in range(harmonics):
            product = modes_at(n) * columns
            if total_columns & (total_columns - 1) == 0:
                turns = product & (total_columns - 1)
            else:
                turns = jnp.remainder(product, total_columns)
            angle = (2.0 * math.pi / total_columns) * turns.astype(jnp.float32)
            made.append((jnp.cos(angle), jnp.sin(angle)))
        return made

    tab_main = [
        (cosine, sign * sine)
        for cosine, sine in tables(
            lambda n: jnp.where(sub < 4, mode_of(row - 1, n), mode_of(row, n)), blk * width + lane
        )
    ]
    part, off = lane // seg, lane % seg
    edge_column = jnp.where(off < 3 * HALO, off - HALO, off + width - 5 * HALO)

    def edge_mode(n):
        lower, upper = mode_of(row - 1, n), mode_of(row, n)
        rising = jnp.where(part == 0, lower, jnp.where(part == layers, upper, 0))
        falling = jnp.where(part == 1, -lower, jnp.where(part == layers + 1, -upper, 0))
        return jnp.where(sub < 4, falling, rising)

    tab_edge = tables(edge_mode, blk * width + edge_column)
    own_rate = FREQ_SCALE * count_of(row)
    next_rate = jnp.where(sub < 4, FREQ_SCALE * count_of(row - 1), FREQ_SCALE * count_of(row + 1))
    own_rates = [own_rate * float(n) for n in range(1, harmonics + 1)]
    edge_rate = jnp.where(
        part == 0,
        FREQ_SCALE * count_of(row - 1),
        jnp.where(part == layers + 1, FREQ_SCALE * count_of(row + 1), own_rate),
    )
    edge_rates = [edge_rate * float(n) for n in range(1, harmonics + 1)]
    next_rates = [next_rate * float(n) for n in range(1, harmonics + 1)]

    fetch.wait()
    fetch_in.wait()

    def shifted(value, by):
        return pltpu.roll(value, by % width, 1)

    def spot_of(item):
        g, m = item // slots, item % slots
        return g, (m % per) * HALO + (m // per) * layers * seg

    for g in range(groups):
        edges = [jnp.zeros(shape, jnp.float32), jnp.zeros(shape, jnp.float32)]
        for k in range(g * slots, min((g + 1) * slots, fields)):
            _, p = spot_of(k)
            for layer in range(layers):
                q = p + layer * seg
                value = e_main[k, PAD + 8 * layer : PAD + 8 * layer + 8, :]
                spot = lane // HALO == q // HALO
                edges[0] = jnp.where(spot, shifted(value, q), edges[0])
                edges[1] = jnp.where(spot, shifted(value, q + HALO), edges[1])
        pack[0, g] = edges[0]
        pack[1, g] = edges[1]
    lane_in = lax.broadcasted_iota(jnp.int32, (nvars, width), 1)
    for c in range(comps):
        g, p = spot_of(fields + c)
        spot = lane_in // HALO == p // HALO
        value = in_main[c]
        pack[0, g, 0:nvars, :] = jnp.where(spot, shifted(value, p), pack[0, g, 0:nvars, :])
        pack[1, g, 0:nvars, :] = jnp.where(spot, shifted(value, p + HALO), pack[1, g, 0:nvars, :])
    for side in range(2):
        for g in range(groups):
            corner[0, side, 2 * g : 2 * g + 2, :] = pack[side, g, 0:2, :]
            corner[1, side, 2 * g : 2 * g + 2, :] = pack[side, g, 6:8, :]

    greeters = 2 + 3 * has_low.astype(jnp.int32) + 3 * has_high.astype(jnp.int32)
    pl.semaphore_wait(barrier, greeters)

    def send(src, dst, index, r, b):
        return pltpu.make_async_remote_copy(
            src_ref=src,
            dst_ref=dst,
            send_sem=send_sem.at[index],
            recv_sem=recv_sem.at[index],
            device_id={"row": r, "blk": b},
            device_id_type=MESH,
        )

    level = [send(pack.at[1], halo.at[0], 0, row, right), send(pack.at[0], halo.at[1], 1, row, left)]
    up = [
        send(corner.at[1, 1], low_halo.at[0], 2, row + 1, right),
        send(corner.at[1, 0], low_halo.at[1], 3, row + 1, left),
        send(state.at[:, pl.ds(depth - 8, 8), :], low, 4, row + 1, blk),
    ]
    down = [
        send(corner.at[0, 1], high_halo.at[0], 5, row - 1, right),
        send(corner.at[0, 0], high_halo.at[1], 6, row - 1, left),
        send(state.at[:, pl.ds(0, 8), :], high, 7, row - 1, blk),
    ]
    for copy in level:
        copy.start()

    @pl.when(has_high)
    def _():
        for copy in up:
            copy.start()

    @pl.when(has_low)
    def _():
        for copy in down:
            copy.start()

    def place(value, where_to):
        at_off = lax.broadcasted_iota(jnp.int32, value.shape, 1) % seg
        start = where_to * seg
        return jnp.where(
            at_off < 3 * HALO,
            shifted(value, start + HALO),
            shifted(value, start + 5 * HALO - width),
        )

    for k in range(fields):
        value = jnp.zeros(shape, jnp.float32)
        for layer in range(layers):
            plane = e_main[k, PAD + 8 * layer : PAD + 8 * layer + 8, :]
            value = jnp.where(part == layer + 1, place(plane, layer + 1), value)
        e_edge[k, 2:10, :] = value
    for c in range(comps):
        in_edge[c] = place(in_main[c], 1)

    @pl.when(has_low)
    def _():
        up[2].wait_recv()
        x_main[:, 0:4, :] = low[:, 4:8, :]
        for k in range(fields):
            e_edge[k, 2:10, :] = jnp.where(part == 0, place(low[k], 0), e_edge[k, 2:10, :])

    @pl.when(jnp.logical_not(has_low))
    def _():
        x_main[:, 0:4, :] = jnp.zeros((fields, 4, width), jnp.float32)

    @pl.when(has_high)
    def _():
        down[2].wait_recv()
        x_main[:, 8:12, :] = high[:, 0:4, :]
        for k in range(fields):
            e_edge[k, 2:10, :] = jnp.where(
                part == layers + 1, place(high[k], layers + 1), e_edge[k, 2:10, :]
            )

    @pl.when(jnp.logical_not(has_high))
    def _():
        x_main[:, 8:12, :] = jnp.zeros((fields, 4, width), jnp.float32)

    def ends(field, inflow_of):
        @pl.when(jnp.logical_not(has_low))
        def _():
            for c in range(comps):
                for v in range(nvars):
                    plane = inflow_of[c, v : v + 1, :]
                    field[c * nvars + v, PAD - 2 : PAD, :] = jnp.broadcast_to(plane, (2, width))

        @pl.when(jnp.logical_not(has_high))
        def _():
            for k in range(fields):
                plane = field[k, PAD + depth - 1 : PAD + depth, :]
                field[k, PAD + depth : PAD + depth + 2, :] = jnp.broadcast_to(plane, (2, width))

    def turn(load, save, table):
        def per_var(v, carry):
            save(v, load(v))
            for n in range(harmonics):
                cosine, sine = table[n]
                real_at, imag_at = (2 * n + 1) * nvars + v, (2 * n + 2) * nvars + v
                real, imag = load(real_at), load(imag_at)
                save(real_at, real * cosine - imag * sine)
                save(imag_at, real * sine + imag * cosine)
            return carry

        lax.fori_loop(0, nvars, per_var, 0)

    def both(e, f, x, y, inflow_of, table, emit):
        x[:, 4:6, :] = e[:, PAD : PAD + 2, :]
        x[:, 6:8, :] = e[:, PAD + depth - 2 : PAD + depth, :]

        def save_first(k, value):
            e[k, PAD - 2 : PAD, :] = value[0:2]
            x[k, 4:8, :] = value[2:6]
            e[k, PAD + depth : PAD + depth + 2, :] = value[6:8]

        turn(lambda k: x[k, 2:10, :], save_first, table)
        ends(e, inflow_of)

        def keep_y(k, value):
            y[k] = value

        def keep_f(k, value):
            f[k, PAD : PAD + depth, :] = value

        section(x, 2, 8, x, 2, 0.5, next_rates, keep_y, comps, nvars)
        section(e, PAD, depth, e, PAD, 0.5, own_rates, keep_f, comps, nvars)

        def save_second(k, value):
            f[k, PAD - 2 : PAD, :] = value[0:2]
            f[k, PAD + depth : PAD + depth + 2, :] = value[6:8]

        turn(lambda k: y[k], save_second, table)
        ends(f, inflow_of)
        section(f, PAD, depth, e, PAD, 1.0, own_rates, emit, comps, nvars)

    def emit_main(k, value):
        out[k] = value

    both(e_main, f_main, x_main, y_main, in_main, tab_main, emit_main)

    for copy in level:
        copy.wait_recv()

    def beyond(value, from_left, from_right, p, start, first, last):
        at_lane = lax.broadcasted_iota(jnp.int32, value.shape, 1)
        at_part, at_off = at_lane // seg, at_lane % seg
        here = jnp.logical_and(at_part >= first, at_part <= last)
        in_left = jnp.logical_and(here, at_off < HALO)
        in_right = jnp.logical_and(here, at_off >= 5 * HALO)
        left_part = shifted(from_left, start - p)
        right_part = shifted(from_right, start + 5 * HALO - p)
        return jnp.where(in_left, left_part, jnp.where(in_right, right_part, value))

    for k in range(fields):
        g, p = spot_of(k)
        e_edge[k, 2:10, :] = beyond(
            e_edge[k, 2:10, :], halo[0, g], halo[1, g], p, seg, 1, layers
        )

    @pl.when(has_low)
    def _():
        up[0].wait_recv()
        up[1].wait_recv()
        for k in range(fields):
            g, p = spot_of(k)
            spot = slice(2 * g, 2 * g + 2)
            e_edge[k, 8:10, :] = beyond(
                e_edge[k, 8:10, :],
                low_halo[0, spot, :],
                low_halo[1, spot, :],
                p + (layers - 1) * seg,
                0,
                0,
                0,
            )

    @pl.when(jnp.logical_not(has_low))
    def _():
        for c in range(comps):
            g, p = spot_of(fields + c)
            in_edge[c] = beyond(
                in_edge[c], halo[0, g, 0:nvars, :], halo[1, g, 0:nvars, :], p, seg, 1, 1
            )

    @pl.when(has_high)
    def _():
        down[0].wait_recv()
        down[1].wait_recv()
        for k in range(fields):
            g, p = spot_of(k)
            spot = slice(2 * g, 2 * g + 2)
            e_edge[k, 2:4, :] = beyond(
                e_edge[k, 2:4, :],
                high_halo[0, spot, :],
                high_halo[1, spot, :],
                p,
                (layers + 1) * seg,
                layers + 1,
                layers + 1,
            )

    def link(field):
        def save(k, value):
            field[k, 0:2, :] = shifted(value, seg)[6:8]
            field[k, 10:12, :] = shifted(value, -seg)[0:2]

        turn(lambda k: field[k, 2:10, :], save, tab_edge)
        two = lax.broadcasted_iota(jnp.int32, (2, width), 1) // seg

        @pl.when(jnp.logical_not(has_low))
        def _():
            for c in range(comps):
                for v in range(nvars):
                    k = c * nvars + v
                    plane = jnp.broadcast_to(in_edge[c, v : v + 1, :], (2, width))
                    field[k, 0:2, :] = jnp.where(two == 1, plane, field[k, 0:2, :])

        @pl.when(jnp.logical_not(has_high))
        def _():
            for k in range(fields):
                plane = jnp.broadcast_to(field[k, 9:10, :], (2, width))
                field[k, 10:12, :] = jnp.where(two == layers, plane, field[k, 10:12, :])

    def keep_edge(k, value):
        f_edge[k, 2:10, :] = value

    def emit_edge(k, value):
        first = lane < HALO
        last = lane >= width - HALO
        outer = jnp.logical_or(first, last)
        for layer in range(layers):
            start = (layer + 1) * seg + HALO
            moved = jnp.where(
                first, shifted(value, -start), shifted(value, width - 4 * HALO - start)
            )
            rows = slice(8 * layer, 8 * layer + 8)
            out[k, rows, :] = jnp.where(outer, moved, out[k, rows, :])

    link(e_edge)
    section(e_edge, 2, 8, e_edge, 2, 0.5, edge_rates, keep_edge, comps, nvars)
    link(f_edge)
    section(f_edge, 2, 8, e_edge, 2, 1.0, edge_rates, emit_edge, comps, nvars)

    for copy in level:
        copy.wait_send()

    @pl.when(has_high)
    def _():
        for copy in up:
            copy.wait_send()

    @pl.when(has_low)
    def _():
        for copy in down:
            copy.wait_send()


def body(rows_total, blocks, state, inflow, blade_counts, modes):
    _, comps, nvars, depth, width = state.shape
    fields = comps * nvars
    _, groups = packing(fields + comps, depth // 8, width)
    corner_rows = -(-2 * groups // 8) * 8
    f32 = jnp.float32

    def buf(*shape):
        return pltpu.VMEM(shape, f32)

    tall = depth + 2 * PAD
    result = pl.pallas_call(
        functools.partial(kernel, rows_total, blocks, nvars),
        out_shape=jax.ShapeDtypeStruct((fields, depth, width), f32),
        in_specs=[
            pl.BlockSpec(memory_space=pltpu.HBM),
            pl.BlockSpec(memory_space=pltpu.HBM),
            pl.BlockSpec(memory_space=pltpu.HBM),
            pl.BlockSpec(memory_space=pltpu.HBM),
        ],
        out_specs=pl.BlockSpec(memory_space=pltpu.VMEM),
        scratch_shapes=[
            buf(fields, tall, width),
            buf(fields, 16, width),
            buf(fields, tall, width),
            buf(fields, 16, width),
            buf(fields, 16, width),
            buf(fields, 8, width),
            buf(comps, nvars, width),
            buf(comps, nvars, width),
            buf(2, groups, 8, width),
            buf(2, 2, corner_rows, width),
            buf(2, groups, 8, width),
            buf(fields, 8, width),
            buf(fields, 8, width),
            buf(2, corner_rows, width),
            buf(2, corner_rows, width),
            pltpu.SMEM(modes.shape, jnp.int32),
            pltpu.SMEM(blade_counts.shape, jnp.int32),
            pltpu.SemaphoreType.DMA((4,)),
            pltpu.SemaphoreType.DMA((8,)),
            pltpu.SemaphoreType.DMA((8,)),
        ],
        compiler_params=pltpu.CompilerParams(
            collective_id=0, has_side_effects=True, vmem_limit_bytes=16 << 20
        ),
    )(
        *(
            pltpu.with_memory_space_constraint(value, pltpu.HBM)
            for value in (modes, blade_counts, state.reshape(fields, depth, width), inflow)
        )
    )
    return result.reshape(1, comps, nvars, depth, width)


def solution(mesh):
    placed = (P("row", None, None, None, "blk"), P(None, None, "blk"), P(), P())
    return jax.shard_map(
        functools.partial(body, mesh.shape["row"], mesh.shape["blk"]),
        mesh=mesh,
        in_specs=placed,
        out_specs=P("row", None, None, None, "blk"),
        check_vma=False,
    )
```

```python
import functools
import math

import jax
import jax.numpy as jnp
from jax import lax
from jax.experimental import pallas as pl
from jax.experimental.pallas import tpu as pltpu
from jax.sharding import PartitionSpec as P

DIFFUSE = 0.05
FOURTH_SMOOTH = 0.03
COURANT = 0.6
FREQ_SCALE = 0.02
MESH = pl.DeviceIdType.MESH
NEAR = DIFFUSE + 4.0 * FOURTH_SMOOTH
CENTER = -4.0 * DIFFUSE - 12.0 * FOURTH_SMOOTH
HALO = 4
PAD = 8


def packing(items, layers, width):
    seg = width // (layers + 2)
    slots = width // (layers * seg) * (seg // HALO)
    return seg, -(-items // slots)


def section(src, base, rows, start, start_base, weight, rates, emit, comps, nvars):
    width = src.shape[2]

    def at(c, v, off):
        return src[c * nvars + v, base + off : base + off + rows, :]

    def opening(v):
        return start[v, start_base : start_base + rows, :]

    coef_up = (NEAR - 0.5) - 0.25 * jnp.tanh(at(0, 1, 1))
    coef_down = (NEAR + 0.5) + 0.25 * jnp.tanh(at(0, 1, -1))
    half_turn = 0.25 * jnp.tanh(at(0, 2, 0))
    coef_next = NEAR - pltpu.roll(half_turn, width - 1, 1)
    coef_prev = NEAR + pltpu.roll(half_turn, 1, 1)
    step = (weight * COURANT) / (
        1.0 + 0.5 * jnp.tanh(opening(1)) + jnp.abs(0.5 * jnp.tanh(opening(2)))
    )

    def one(c, v):
        here, up, down = at(c, v, 0), at(c, v, 1), at(c, v, -1)
        far = (
            at(c, v, 2)
            + at(c, v, -2)
            + pltpu.roll(here, width - 2, 1)
            + pltpu.roll(here, 2, 1)
        )
        total = (
            coef_up * up
            + coef_down * down
            + coef_next * pltpu.roll(here, width - 1, 1)
            + coef_prev * pltpu.roll(here, 1, 1)
            + CENTER * here
            - FOURTH_SMOOTH * far
        )
        return here, up, down, total

    def put(c, v, total):
        k = c * nvars + v
        emit(k, start[k, start_base : start_base + rows, :] + step * total)

    def per_var(v, carry):
        stress = None
        for n in range(1, comps // 2 + 1):
            real, real_up, real_down, real_total = one(2 * n - 1, v)
            imag, imag_up, imag_down, imag_total = one(2 * n, v)
            rate = rates[n - 1]
            put(2 * n - 1, v, real_total + rate * imag)
            put(2 * n, v, imag_total - rate * real)
            term = (
                at(2 * n - 1, 1, 1) * real_up
                + at(2 * n, 1, 1) * imag_up
                - at(2 * n - 1, 1, -1) * real_down
                - at(2 * n, 1, -1) * imag_down
            )
            stress = term if stress is None else stress + term
        _, _, _, total = one(0, v)
        put(0, v, total - 0.25 * stress)
        return carry

    lax.fori_loop(0, nvars, per_var, 0, unroll=True)


def kernel(
    rows_total,
    blocks,
    nvars,
    modes_in,
    counts_in,
    state,
    inflow,
    out,
    e_main,
    e_edge,
    f_main,
    f_edge,
    x_main,
    y_main,
    in_main,
    in_edge,
    pack,
    corner,
    halo,
    low,
    high,
    low_halo,
    high_halo,
    modes,
    counts,
    local_sem,
    send_sem,
    recv_sem,
):
    fields, depth, width = state.shape
    comps = fields // nvars
    harmonics = comps // 2
    layers = depth // 8
    seg, groups = packing(fields + comps, layers, width)
    per = seg // HALO
    slots = width // (layers * seg) * per
    total_columns = width * blocks
    row = lax.axis_index("row")
    blk = lax.axis_index("blk")
    right = lax.rem(blk + 1, blocks)
    left = lax.rem(blk + blocks - 1, blocks)
    has_low = row > 0
    has_high = row < rows_total - 1

    barrier = pltpu.get_barrier_semaphore()

    def greet(r, b):
        pl.semaphore_signal(barrier, inc=1, device_id={"row": r, "blk": b}, device_id_type=MESH)

    greet(row, right)
    greet(row, left)

    @pl.when(has_high)
    def _():
        greet(row + 1, right)
        greet(row + 1, left)
        greet(row + 1, blk)

    @pl.when(has_low)
    def _():
        greet(row - 1, right)
        greet(row - 1, left)
        greet(row - 1, blk)

    fetch = pltpu.make_async_copy(state, e_main.at[:, PAD : PAD + depth, :], local_sem.at[0])
    fetch_in = pltpu.make_async_copy(inflow, in_main, local_sem.at[1])
    fetch_modes = pltpu.make_async_copy(modes_in, modes, local_sem.at[2])
    fetch_counts = pltpu.make_async_copy(counts_in, counts, local_sem.at[3])
    for copy in (fetch, fetch_in, fetch_modes, fetch_counts):
        copy.start()

    shape = (8, width)
    sub = lax.broadcasted_iota(jnp.int32, shape, 0)
    lane = lax.broadcasted_iota(jnp.int32, shape, 1)
    part, off = lane // seg, lane % seg
    fetch.wait()
    fetch_in.wait()

    def shifted(value, by):
        return pltpu.roll(value, by % width, 1)

    def spot_of(item):
        g, m = item // slots, item % slots
        return g, (m % per) * HALO + (m // per) * layers * seg

    for g in range(groups):
        edges = [jnp.zeros(shape, jnp.float32), jnp.zeros(shape, jnp.float32)]
        for k in range(g * slots, min((g + 1) * slots, fields)):
            _, p = spot_of(k)
            for layer in range(layers):
                q = p + layer * seg
                value = e_main[k, PAD + 8 * layer : PAD + 8 * layer + 8, :]
                spot = lane // HALO == q // HALO
                edges[0] = jnp.where(spot, shifted(value, q), edges[0])
                edges[1] = jnp.where(spot, shifted(value, q + HALO), edges[1])
        pack[0, g] = edges[0]
        pack[1, g] = edges[1]
    lane_in = lax.broadcasted_iota(jnp.int32, (nvars, width), 1)
    for c in range(comps):
        g, p = spot_of(fields + c)
        spot = lane_in // HALO == p // HALO
        value = in_main[c]
        pack[0, g, 0:nvars, :] = jnp.where(spot, shifted(value, p), pack[0, g, 0:nvars, :])
        pack[1, g, 0:nvars, :] = jnp.where(spot, shifted(value, p + HALO), pack[1, g, 0:nvars, :])
    for side in range(2):
        for g in range(groups):
            corner[0, side, 2 * g : 2 * g + 2, :] = pack[side, g, 0:2, :]
            corner[1, side, 2 * g : 2 * g + 2, :] = pack[side, g, 6:8, :]

    greeters = 2 + 3 * has_low.astype(jnp.int32) + 3 * has_high.astype(jnp.int32)
    pl.semaphore_wait(barrier, greeters)

    def send(src, dst, index, r, b):
        return pltpu.make_async_remote_copy(
            src_ref=src,
            dst_ref=dst,
            send_sem=send_sem.at[index],
            recv_sem=recv_sem.at[index],
            device_id={"row": r, "blk": b},
            device_id_type=MESH,
        )

    level = [send(pack.at[1], halo.at[0], 0, row, right), send(pack.at[0], halo.at[1], 1, row, left)]
    up = [
        send(corner.at[1, 1], low_halo.at[0], 2, row + 1, right),
        send(corner.at[1, 0], low_halo.at[1], 3, row + 1, left),
        send(state.at[:, pl.ds(depth - 8, 8), :], low, 4, row + 1, blk),
    ]
    down = [
        send(corner.at[0, 1], high_halo.at[0], 5, row - 1, right),
        send(corner.at[0, 0], high_halo.at[1], 6, row - 1, left),
        send(state.at[:, pl.ds(0, 8), :], high, 7, row - 1, blk),
    ]
    for copy in level:
        copy.start()

    @pl.when(has_high)
    def _():
        for copy in up:
            copy.start()

    @pl.when(has_low)
    def _():
        for copy in down:
            copy.start()

    def place(value, where_to):
        at_off = lax.broadcasted_iota(jnp.int32, value.shape, 1) % seg
        start = where_to * seg
        return jnp.where(
            at_off < 3 * HALO,
            shifted(value, start + HALO),
            shifted(value, start + 5 * HALO - width),
        )

    for k in range(fields):
        value = jnp.zeros(shape, jnp.float32)
        for layer in range(layers):
            plane = e_main[k, PAD + 8 * layer : PAD + 8 * layer + 8, :]
            value = jnp.where(part == layer + 1, place(plane, layer + 1), value)
        e_edge[k, 2:10, :] = value
    for c in range(comps):
        in_edge[c] = place(in_main[c], 1)

    fetch_modes.wait()
    fetch_counts.wait()
    sign = jnp.where((sub // 2) % 2 == 0, 1.0, -1.0).astype(jnp.float32)

    def mode_of(interface, n):
        value = jnp.int32(0)
        for i in range(rows_total - 1):
            value = value + jnp.where(interface == i, modes[i, n], 0)
        return value

    def count_of(wanted):
        value = jnp.int32(0)
        for i in range(rows_total):
            value = value + jnp.where(wanted == i, counts[i], 0)
        return value.astype(jnp.float32)

    def tables(modes_at, columns):
        made = []
        for n in range(harmonics):
            product = modes_at(n) * columns
            if total_columns & (total_columns - 1) == 0:
                turns = product & (total_columns - 1)
            else:
                turns = jnp.remainder(product, total_columns)
            angle = (2.0 * math.pi / total_columns) * turns.astype(jnp.float32)
            made.append((jnp.cos(angle), jnp.sin(angle)))
        return made

    tab_main = [
        (cosine, sign * sine)
        for cosine, sine in tables(
            lambda n: jnp.where(sub < 4, mode_of(row - 1, n), mode_of(row, n)), blk * width + lane
        )
    ]
    edge_column = jnp.where(off < 3 * HALO, off - HALO, off + width - 5 * HALO)

    def edge_mode(n):
        lower, upper = mode_of(row - 1, n), mode_of(row, n)
        rising = jnp.where(part == 0, lower, jnp.where(part == layers, upper, 0))
        falling = jnp.where(part == 1, -lower, jnp.where(part == layers + 1, -upper, 0))
        return jnp.where(sub < 4, falling, rising)

    tab_edge = tables(edge_mode, blk * width + edge_column)
    own_rate = FREQ_SCALE * count_of(row)
    next_rate = jnp.where(sub < 4, FREQ_SCALE * count_of(row - 1), FREQ_SCALE * count_of(row + 1))
    own_rates = [own_rate * float(n) for n in range(1, harmonics + 1)]
    edge_rate = jnp.where(
        part == 0,
        FREQ_SCALE * count_of(row - 1),
        jnp.where(part == layers + 1, FREQ_SCALE * count_of(row + 1), own_rate),
    )
    edge_rates = [edge_rate * float(n) for n in range(1, harmonics + 1)]
    next_rates = [next_rate * float(n) for n in range(1, harmonics + 1)]

    @pl.when(has_low)
    def _():
        up[2].wait_recv()
        x_main[:, 0:4, :] = low[:, 4:8, :]
        for k in range(fields):
            e_edge[k, 2:10, :] = jnp.where(part == 0, place(low[k], 0), e_edge[k, 2:10, :])

    @pl.when(jnp.logical_not(has_low))
    def _():
        x_main[:, 0:4, :] = jnp.zeros((fields, 4, width), jnp.float32)

    @pl.when(has_high)
    def _():
        down[2].wait_recv()
        x_main[:, 8:12, :] = high[:, 0:4, :]
        for k in range(fields):
            e_edge[k, 2:10, :] = jnp.where(
                part == layers + 1, place(high[k], layers + 1), e_edge[k, 2:10, :]
            )

    @pl.when(jnp.logical_not(has_high))
    def _():
        x_main[:, 8:12, :] = jnp.zeros((fields, 4, width), jnp.float32)

    def ends(field, inflow_of):
        @pl.when(jnp.logical_not(has_low))
        def _():
            for c in range(comps):
                for v in range(nvars):
                    plane = inflow_of[c, v : v + 1, :]
                    field[c * nvars + v, PAD - 2 : PAD, :] = jnp.broadcast_to(plane, (2, width))

        @pl.when(jnp.logical_not(has_high))
        def _():
            for k in range(fields):
                plane = field[k, PAD + depth - 1 : PAD + depth, :]
                field[k, PAD + depth : PAD + depth + 2, :] = jnp.broadcast_to(plane, (2, width))

    def turn(load, save, table):
        def per_var(v, carry):
            save(v, load(v))
            for n in range(harmonics):
                cosine, sine = table[n]
                real_at, imag_at = (2 * n + 1) * nvars + v, (2 * n + 2) * nvars + v
                real, imag = load(real_at), load(imag_at)
                save(real_at, real * cosine - imag * sine)
                save(imag_at, real * sine + imag * cosine)
            return carry

        lax.fori_loop(0, nvars, per_var, 0, unroll=True)

    def both(e, f, x, y, inflow_of, table, emit):
        x[:, 4:6, :] = e[:, PAD : PAD + 2, :]
        x[:, 6:8, :] = e[:, PAD + depth - 2 : PAD + depth, :]

        def save_first(k, value):
            e[k, PAD - 2 : PAD, :] = value[0:2]
            x[k, 4:8, :] = value[2:6]
            e[k, PAD + depth : PAD + depth + 2, :] = value[6:8]

        turn(lambda k: x[k, 2:10, :], save_first, table)
        ends(e, inflow_of)

        def keep_y(k, value):
            y[k] = value

        def keep_f(k, value):
            f[k, PAD : PAD + depth, :] = value

        section(x, 2, 8, x, 2, 0.5, next_rates, keep_y, comps, nvars)
        section(e, PAD, depth, e, PAD, 0.5, own_rates, keep_f, comps, nvars)

        def save_second(k, value):
            f[k, PAD - 2 : PAD, :] = value[0:2]
            f[k, PAD + depth : PAD + depth + 2, :] = value[6:8]

        turn(lambda k: y[k], save_second, table)
        ends(f, inflow_of)
        section(f, PAD, depth, e, PAD, 1.0, own_rates, emit, comps, nvars)

    def emit_main(k, value):
        out[k] = value

    both(e_main, f_main, x_main, y_main, in_main, tab_main, emit_main)

    for copy in level:
        copy.wait_recv()

    def beyond(value, from_left, from_right, p, start, first, last):
        at_lane = lax.broadcasted_iota(jnp.int32, value.shape, 1)
        at_part, at_off = at_lane // seg, at_lane % seg
        here = jnp.logical_and(at_part >= first, at_part <= last)
        in_left = jnp.logical_and(here, at_off < HALO)
        in_right = jnp.logical_and(here, at_off >= 5 * HALO)
        left_part = shifted(from_left, start - p)
        right_part = shifted(from_right, start + 5 * HALO - p)
        return jnp.where(in_left, left_part, jnp.where(in_right, right_part, value))

    for k in range(fields):
        g, p = spot_of(k)
        e_edge[k, 2:10, :] = beyond(
            e_edge[k, 2:10, :], halo[0, g], halo[1, g], p, seg, 1, layers
        )

    @pl.when(has_low)
    def _():
        up[0].wait_recv()
        up[1].wait_recv()
        for k in range(fields):
            g, p = spot_of(k)
            spot = slice(2 * g, 2 * g + 2)
            e_edge[k, 8:10, :] = beyond(
                e_edge[k, 8:10, :],
                low_halo[0, spot, :],
                low_halo[1, spot, :],
                p + (layers - 1) * seg,
                0,
                0,
                0,
            )

    @pl.when(jnp.logical_not(has_low))
    def _():
        for c in range(comps):
            g, p = spot_of(fields + c)
            in_edge[c] = beyond(
                in_edge[c], halo[0, g, 0:nvars, :], halo[1, g, 0:nvars, :], p, seg, 1, 1
            )

    @pl.when(has_high)
    def _():
        down[0].wait_recv()
        down[1].wait_recv()
        for k in range(fields):
            g, p = spot_of(k)
            spot = slice(2 * g, 2 * g + 2)
            e_edge[k, 2:4, :] = beyond(
                e_edge[k, 2:4, :],
                high_halo[0, spot, :],
                high_halo[1, spot, :],
                p,
                (layers + 1) * seg,
                layers + 1,
                layers + 1,
            )

    def link(field):
        def save(k, value):
            field[k, 0:2, :] = shifted(value, seg)[6:8]
            field[k, 10:12, :] = shifted(value, -seg)[0:2]

        turn(lambda k: field[k, 2:10, :], save, tab_edge)
        two = lax.broadcasted_iota(jnp.int32, (2, width), 1) // seg

        @pl.when(jnp.logical_not(has_low))
        def _():
            for c in range(comps):
                for v in range(nvars):
                    k = c * nvars + v
                    plane = jnp.broadcast_to(in_edge[c, v : v + 1, :], (2, width))
                    field[k, 0:2, :] = jnp.where(two == 1, plane, field[k, 0:2, :])

        @pl.when(jnp.logical_not(has_high))
        def _():
            for k in range(fields):
                plane = jnp.broadcast_to(field[k, 9:10, :], (2, width))
                field[k, 10:12, :] = jnp.where(two == layers, plane, field[k, 10:12, :])

    def keep_edge(k, value):
        f_edge[k, 2:10, :] = value

    def emit_edge(k, value):
        first = lane < HALO
        last = lane >= width - HALO
        outer = jnp.logical_or(first, last)
        for layer in range(layers):
            start = (layer + 1) * seg + HALO
            moved = jnp.where(
                first, shifted(value, -start), shifted(value, width - 4 * HALO - start)
            )
            rows = slice(8 * layer, 8 * layer + 8)
            out[k, rows, :] = jnp.where(outer, moved, out[k, rows, :])

    link(e_edge)
    section(e_edge, 2, 8, e_edge, 2, 0.5, edge_rates, keep_edge, comps, nvars)
    link(f_edge)
    section(f_edge, 2, 8, e_edge, 2, 1.0, edge_rates, emit_edge, comps, nvars)

    for copy in level:
        copy.wait_send()

    @pl.when(has_high)
    def _():
        for copy in up:
            copy.wait_send()

    @pl.when(has_low)
    def _():
        for copy in down:
            copy.wait_send()


def body(rows_total, blocks, state, inflow, blade_counts, modes):
    _, comps, nvars, depth, width = state.shape
    fields = comps * nvars
    _, groups = packing(fields + comps, depth // 8, width)
    corner_rows = -(-2 * groups // 8) * 8
    f32 = jnp.float32

    def buf(*shape):
        return pltpu.VMEM(shape, f32)

    tall = depth + 2 * PAD
    result = pl.pallas_call(
        functools.partial(kernel, rows_total, blocks, nvars),
        out_shape=jax.ShapeDtypeStruct((fields, depth, width), f32),
        in_specs=[
            pl.BlockSpec(memory_space=pltpu.HBM),
            pl.BlockSpec(memory_space=pltpu.HBM),
            pl.BlockSpec(memory_space=pltpu.HBM),
            pl.BlockSpec(memory_space=pltpu.HBM),
        ],
        out_specs=pl.BlockSpec(memory_space=pltpu.VMEM),
        scratch_shapes=[
            buf(fields, tall, width),
            buf(fields, 16, width),
            buf(fields, tall, width),
            buf(fields, 16, width),
            buf(fields, 16, width),
            buf(fields, 8, width),
            buf(comps, nvars, width),
            buf(comps, nvars, width),
            buf(2, groups, 8, width),
            buf(2, 2, corner_rows, width),
            buf(2, groups, 8, width),
            buf(fields, 8, width),
            buf(fields, 8, width),
            buf(2, corner_rows, width),
            buf(2, corner_rows, width),
            pltpu.SMEM(modes.shape, jnp.int32),
            pltpu.SMEM(blade_counts.shape, jnp.int32),
            pltpu.SemaphoreType.DMA((4,)),
            pltpu.SemaphoreType.DMA((8,)),
            pltpu.SemaphoreType.DMA((8,)),
        ],
        compiler_params=pltpu.CompilerParams(
            collective_id=0, has_side_effects=True, vmem_limit_bytes=16 << 20
        ),
    )(
        *(
            pltpu.with_memory_space_constraint(value, pltpu.HBM)
            for value in (modes, blade_counts, state.reshape(fields, depth, width), inflow)
        )
    )
    return result.reshape(1, comps, nvars, depth, width)


def solution(mesh):
    placed = (P("row", None, None, None, "blk"), P(None, None, "blk"), P(), P())
    return jax.shard_map(
        functools.partial(body, mesh.shape["row"], mesh.shape["blk"]),
        mesh=mesh,
        in_specs=placed,
        out_specs=P("row", None, None, None, "blk"),
        check_vma=False,
    )
```
